32 devices in a mesh: groups: 2 (over y), ctx: 4 (over z), head: 2 (over x), pair: 2 (over core).
Axes of the slice: x: 2, y: 2, z: 4, core: 2. Of those that a mesh axis runs over, the one named last changes fastest.
Arguments:
- q_raw: bfloat16 [4096, 2048], P(('groups', 'ctx', 'pair'), 'head'), parts along dimension 0, may hold values from -6 to 6
- k_raw: bfloat16 [4096, 2048], P(('groups', 'ctx', 'pair'), 'head'), parts along dimension 0, may hold values from -6 to 6
- v_raw: bfloat16 [4096, 4096], P(('groups', 'ctx', 'pair'), 'head'), parts along dimension 0, may hold values from -6 to 6
- beta_logit: bfloat16 [32, 4096], P('head', ('groups', 'ctx', 'pair')), parts along dimension 1, may hold values from -6 to 6
- gate_logit: bfloat16 [32, 4096], P('head', ('groups', 'ctx', 'pair')), parts along dimension 1, may hold values from -4 to 13
- out_grad: bfloat16 [4096, 4096], P(('groups', 'ctx', 'pair'), 'head'), parts along dimension 0, may hold values from -6 to 6
- conv_q: bfloat16 [4, 2048], P(None, 'head'), may hold values from -3 to 3
- conv_k: bfloat16 [4, 2048], P(None, 'head'), may hold values from -3 to 3
- conv_v: bfloat16 [4, 4096], P(None, 'head'), may hold values from -3 to 3
- a_log: float32 [32], P('head'), may hold values from 0 to 2.77
- dt_bias: float32 [32], P('head'), may hold values from -16 to -2.9
- doc_ids: int32 [4096], P(('groups', 'ctx', 'pair')), parts along dimension 0, may hold values from 0 to 7, never falling along the last dimension, each value on 1 to 512 neighbouring positions
- swap_blocks: int32 [8], P(('groups', 'ctx')), parts along dimension 0, may hold values from 0 to 1, as said below
Outputs:
- layer_out: bfloat16 [4096, 4096], P(('groups', 'ctx', 'pair'), 'head'), parts along dimension 0
- q_grad: bfloat16 [4096, 2048], P(('groups', 'ctx', 'pair'), 'head'), parts along dimension 0
- k_grad: bfloat16 [4096, 2048], P(('groups', 'ctx', 'pair'), 'head'), parts along dimension 0
- v_grad: bfloat16 [4096, 4096], P(('groups', 'ctx', 'pair'), 'head'), parts along dimension 0
- beta_grad: bfloat16 [32, 4096], P('head', ('groups', 'ctx', 'pair')), parts along dimension 1
- gate_grad: bfloat16 [32, 4096], P('head', ('groups', 'ctx', 'pair')), parts along dimension 1
The draws below stay inside these ranges and needn't reach their ends.
There are 2 independent parts, one for each index of `groups`. The reference program is written for one: setup_inputs(seed, part) draws one part's arguments, and reference() takes and returns one part's arrays. A program takes and returns all parts, laid end to end along the dimension named above; an argument that names none is the same for every part. Nothing has to cross between parts.
Inputs may be any that keep to these rules, and one draw needn't show every extreme that they name: `doc_ids`: document numbers start at 0 and never fall along the tokens; each document has 1 to 512 tokens, one exactly 512. `swap_blocks`: 1 occurs at some context index.
All inputs are finite; a program needn't handle non-finite values.
Results may differ from the reference program's by a relative error of at most 0.001.
Values may be sent and summed in bfloat16 or wider, within the bound.
A program may use at most 320 MiB of HBM per device.

```python
import math
import jax
import jax.numpy as jnp
import numpy as np
from jax import lax

HK = 16
OUTPUT_GROUPS = 32
DK = 128
DV = 128
TAPS = 4
CH = 128
SWAP = 128
DOCS = 8
SHARD_TOKENS = 256
MAXB = 1
CTXS = 4
SPAN_POSITIONS = 2048
DOCMAX = 512
N_CTX = 4
N_PAIR = 2


def draw_dt_bias(key, part):
    first_key = jax.random.fold_in(key, 0)
    result = jax.random.uniform(first_key, (OUTPUT_GROUPS,), jnp.float32, math.log(0.05 / SPAN_POSITIONS), math.log(0.05))
    return result.astype(jnp.float32)


def draw_gate_logit(key, part):
    first_key, next_address, third_key = jax.random.split(key, 3)
    initial_entries = 0.5 * jax.random.normal(first_key, (OUTPUT_GROUPS, SPAN_POSITIONS), jnp.float32)
    position_runs = jax.random.uniform(next_address, (OUTPUT_GROUPS, SPAN_POSITIONS), jnp.float32) < 4.0 / SPAN_POSITIONS
    tier_sizes = jax.random.uniform(third_key, (OUTPUT_GROUPS, SPAN_POSITIONS), jnp.float32, 10.0, 13.0)
    return jnp.where(position_runs, tier_sizes, jnp.clip(initial_entries, -3.9, 3.9)).astype(jnp.bfloat16)


def draw_swap_blocks(key, part):
    first_key, next_address = jax.random.split(key)
    counts = jax.random.randint(first_key, (CTXS,), 0, MAXB + 1)
    where_most = jax.random.randint(next_address, (), 0, CTXS)
    positions = jnp.arange(CTXS)
    return jnp.where(positions == where_most, MAXB, counts).astype(jnp.int32)


def level_of(own_key, dims, cuts, least, high):
    def one(dim, blocks):
        steps = jax.random.uniform(jax.random.fold_in(jax.random.fold_in(own_key, 6), dim), (blocks,), jnp.float32, least / len(cuts), high / len(cuts))
        return jnp.repeat(jnp.exp(steps), dims[dim] // blocks).reshape((-1,) + (1,) * (len(dims) - dim - 1))

    level = one(*cuts[0])
    for cut in cuts[1:]:
        level = level * one(*cut)
    return level


def profile(count, total, limit, lean):
    portions = [(1 << 20) // math.isqrt(rank ** lean) + 1 for rank in range(2, count + 1)]
    surplus, given = total - limit - (count - 1), [1] * (count - 1)
    while surplus > 0:
        movable = [i for i in range(count - 1) if given[i] < limit]
        whole, budget = sum([portions[i] for i in movable]), surplus
        for i in movable:
            more = min(limit - given[i], max(1, budget * portions[i] // whole), surplus)
            given[i] = given[i] + more
            surplus = surplus - more
    return np.array([limit] + given)


def ragged_sizes(rng, amount, total, bound, skew):
    if amount == 2:
        one = jax.random.randint(rng, (), max(1, total - bound), min(bound, total - 1) + 1)
        return jnp.stack([one, total - one])
    sizes = jnp.asarray(profile(amount, total, bound, skew), jnp.int32)
    twos = (amount - 1) // 2
    source_of, taker = sizes[1:1 + 2 * twos:2], sizes[2:2 + 2 * twos:2]
    slack = jnp.minimum(source_of - 1, bound - taker)
    shifted = jax.random.randint(jax.random.fold_in(rng, 1), (twos,), 0, 1 << 20) % (slack + 1)
    sizes = sizes.at[1:1 + 2 * twos:2].set(source_of - shifted).at[2:2 + 2 * twos:2].set(taker + shifted)
    return sizes[jax.random.permutation(jax.random.fold_in(rng, 2), amount)]


def scatter_about(stream_key, dims, deviation, limit, cuts=(), kind=jnp.bfloat16):
    values = deviation * jax.random.normal(stream_key, dims, jnp.float32)
    if cuts:
        values = values * level_of(stream_key, dims, cuts, -0.22, 0.18)
    return jnp.clip(values, -limit, limit).astype(kind)


def setup_inputs(seed: int = 0, part: int = 0) -> dict:
    streams_of = jax.random.split(jax.random.key(seed), 14)
    part_splits = jax.random.split(jax.random.fold_in(streams_of[13], part), 14)
    return {
        "q_raw": scatter_about(part_splits[0], (SPAN_POSITIONS, HK * DK), 1.0, 6.0, ((0, 8), (1, 2))),
        "k_raw": scatter_about(part_splits[1], (SPAN_POSITIONS, HK * DK), 1.0, 6.0, ((0, 8), (1, 2))),
        "v_raw": scatter_about(part_splits[2], (SPAN_POSITIONS, OUTPUT_GROUPS * DV), 1.0, 6.0, ((0, 8), (1, 2))),
        "beta_logit": scatter_about(part_splits[3], (OUTPUT_GROUPS, SPAN_POSITIONS), 1.5, 6.0, ((0, 2), (1, 8))),
        "gate_logit": draw_gate_logit(jax.random.fold_in(jax.random.fold_in(streams_of[13], part), 71), part),
        "out_grad": scatter_about(part_splits[5], (SPAN_POSITIONS, OUTPUT_GROUPS * DV), 1.0, 6.0, ((0, 8), (1, 2))),
        "conv_q": scatter_about(streams_of[6], (TAPS, HK * DK), TAPS ** -0.5, 3.0, ((1, 2),)),
        "conv_k": scatter_about(streams_of[7], (TAPS, HK * DK), TAPS ** -0.5, 3.0, ((1, 2),)),
        "conv_v": scatter_about(streams_of[8], (TAPS, OUTPUT_GROUPS * DV), TAPS ** -0.5, 3.0, ((1, 2),)),
        "a_log": jnp.clip(2.77 * jax.random.uniform(streams_of[9], (OUTPUT_GROUPS,), jnp.float32) ** level_of(streams_of[9], (OUTPUT_GROUPS,), ((0, 2),), -0.2, 0.2), 0.0, 2.77),
        "dt_bias": draw_dt_bias(jax.random.fold_in(streams_of[13], 71), part),
        "doc_ids": jnp.searchsorted(jnp.cumsum(ragged_sizes(part_splits[11], DOCS, SPAN_POSITIONS, DOCMAX, 0)), jnp.arange(SPAN_POSITIONS), side="right").astype(jnp.int32),
        "swap_blocks": draw_swap_blocks(jax.random.fold_in(jax.random.fold_in(streams_of[13], part), 71), part),
    }


highest = lax.Precision.HIGHEST
normalizer_guard = 1e-06

def product(left_matrix, right_matrix):
    return jnp.matmul(left_matrix, right_matrix, precision=highest)

def lower_solve(strict_lower, right_side):
    return jax.scipy.linalg.solve_triangular(strict_lower, right_side, lower=True, unit_diagonal=True)

def conv_silu(extended, weight, ext_ids):
    tap_count = weight.shape[0]
    out_rows = extended.shape[0] - tap_count + 1
    current = ext_ids[tap_count - 1:]
    summed = jnp.zeros((out_rows, extended.shape[1]), jnp.float32)
    for tap_index in range(tap_count):
        same_doc = (ext_ids[tap_index:tap_index + out_rows] == current).astype(jnp.float32)
        summed = summed + weight[tap_index].astype(jnp.float32) * extended[tap_index:tap_index + out_rows] * same_doc[:, None]
    return jax.nn.silu(summed)

def unit_rows(values, head_width):
    shaped = values.reshape(values.shape[0], -1, head_width)
    return shaped / jnp.sqrt(lax.optimization_barrier(jnp.sum(shaped * shaped, axis=-1, keepdims=True)) + normalizer_guard)

def span_pieces(queries, key_rows, values, beta_rate, decay_log, doc_index, before_doc):
    span_len = queries.shape[0]
    positions = jnp.arange(span_len)
    at_or_below = positions[:, None] >= positions[None, :]
    strictly_below = positions[:, None] > positions[None, :]
    cumulative = jnp.cumsum(decay_log)
    same_doc = (doc_index[:, None] == doc_index[None, :]) & at_or_below
    decay_table = jnp.where(same_doc, jnp.exp(jnp.where(same_doc, cumulative[:, None] - cumulative[None, :], 0.0)), 0.0)
    start_decay = jnp.where(doc_index == before_doc, jnp.exp(cumulative), 0.0)
    strict_part = jnp.where(strictly_below, beta_rate[:, None] * decay_table * product(key_rows, key_rows.T), 0.0)
    right_side = jnp.concatenate([beta_rate[:, None] * values, (beta_rate * start_decay)[:, None] * key_rows], axis=1)
    solved = lower_solve(strict_part, right_side)
    scores = decay_table * product(queries, key_rows.T)
    weighted = key_rows * decay_table[span_len - 1][:, None]
    value_width = values.shape[1]
    return (scores, solved[:, :value_width], solved[:, value_width:], start_decay, queries, weighted)

def span_step(carried, pieces):
    scores, base_update, correction, start_decay, queries, weighted = pieces
    updates = base_update - product(correction, carried)
    outputs = start_decay[:, None] * product(queries, carried) + product(scores, updates)
    new_state = start_decay[-1] * carried + product(weighted.T, updates)
    return (new_state, outputs)

def sequence_order(source, blocks, token_axis):
    moved_axis = jnp.moveaxis(source, token_axis, 0)
    shaped = moved_axis.reshape((N_CTX, N_PAIR, SHARD_TOKENS) + moved_axis.shape[1:])

    def fix_pair(couple_lines, block_count):
        first_shard = couple_lines[0]
        second_shard = couple_lines[1]
        moved_rows = (block_count * SWAP).astype(jnp.int32)
        positions = jnp.arange(SHARD_TOKENS, dtype=jnp.int32).reshape((SHARD_TOKENS,) + (1,) * (first_shard.ndim - 1))
        new_first = jnp.where(positions >= SHARD_TOKENS - moved_rows, jnp.roll(second_shard, SHARD_TOKENS - moved_rows, axis=0), first_shard)
        new_second = jnp.where(positions < moved_rows, jnp.roll(first_shard, moved_rows, axis=0), second_shard)
        return jnp.stack([new_first, new_second])
    repaired = jax.vmap(fix_pair)(shaped, blocks)
    return jnp.moveaxis(repaired.reshape(moved_axis.shape), 0, token_axis)

def reference(q_raw, k_raw, v_raw, beta_logit, gate_logit, out_grad, conv_q, conv_k, conv_v, a_log, dt_bias, doc_ids, swap_blocks):
    q_seq = sequence_order(q_raw, swap_blocks, 0)
    k_seq = sequence_order(k_raw, swap_blocks, 0)
    v_seq = sequence_order(v_raw, swap_blocks, 0)
    grad_seq = sequence_order(out_grad, swap_blocks, 0)
    beta_seq = sequence_order(beta_logit, swap_blocks, 1)
    gate_seq = sequence_order(gate_logit, swap_blocks, 1)
    ids_float = doc_ids.astype(jnp.float32)
    ext_ids = jnp.concatenate([jnp.full((TAPS - 1,), -1.0, jnp.float32), ids_float])
    length_all = ids_float.shape[0]
    spans = length_all // CH
    doc_now = ids_float.reshape(spans, CH)
    doc_before = ext_ids[TAPS - 2:TAPS - 2 + length_all:CH]

    def extend(rows_in):
        return jnp.concatenate([jnp.zeros((TAPS - 1, rows_in.shape[1]), jnp.float32), rows_in], axis=0)

    def forward(query_raw, key_raw, value_raw, beta_in, gate_in):
        queries = unit_rows(conv_silu(extend(query_raw), conv_q, ext_ids), DK) / math.sqrt(DK)
        key_rows = unit_rows(conv_silu(extend(key_raw), conv_k, ext_ids), DK)
        value_rows = conv_silu(extend(value_raw), conv_v, ext_ids).reshape(length_all, OUTPUT_GROUPS, DV)
        group_size = OUTPUT_GROUPS // HK
        queries = jnp.repeat(queries, group_size, axis=1).transpose(1, 0, 2)
        key_rows = jnp.repeat(key_rows, group_size, axis=1).transpose(1, 0, 2)
        value_rows = value_rows.transpose(1, 0, 2)
        beta_rate = jax.nn.sigmoid(beta_in)
        decay_log = -jnp.exp(a_log)[:, None] * jax.nn.softplus(gate_in + dt_bias[:, None])

        def one_head(head_inputs):
            head_query, head_key, head_value, head_beta, head_decay = head_inputs
            pieces = jax.vmap(span_pieces)(head_query.reshape(spans, CH, DK), head_key.reshape(spans, CH, DK), head_value.reshape(spans, CH, DV), head_beta.reshape(spans, CH), head_decay.reshape(spans, CH), doc_now, doc_before)
            final_state, outputs = lax.scan(span_step, jnp.zeros((DK, DV), jnp.float32), pieces)
            return outputs.reshape(length_all, DV)
        heads_out = lax.map(jax.checkpoint(one_head), (queries, key_rows, value_rows, beta_rate, decay_log))
        return heads_out.transpose(1, 0, 2).reshape(length_all, OUTPUT_GROUPS * DV)
    outputs, pullback = jax.vjp(forward, q_seq.astype(jnp.float32), k_seq.astype(jnp.float32), v_seq.astype(jnp.float32), beta_seq.astype(jnp.float32), gate_seq.astype(jnp.float32))
    grads = pullback(grad_seq.astype(jnp.float32))
    return (outputs.astype(jnp.bfloat16), grads[0].astype(jnp.bfloat16), grads[1].astype(jnp.bfloat16), grads[2].astype(jnp.bfloat16), grads[3].astype(jnp.bfloat16), grads[4].astype(jnp.bfloat16))
```

```python
import functools
import math

import jax
import jax.numpy as jnp
from jax import lax
from jax.experimental import pallas as pl
from jax.experimental.pallas import tpu as pltpu
from jax.sharding import PartitionSpec as P

DK = 128
TAPS = 4
CH = 128
SWAP = 128
HALO = 8
GUARD = 1e-06
SCALE = 1.0 / math.sqrt(DK)
DOC_PARTS = 4

f32 = jnp.float32
bf16 = jnp.bfloat16
highest = lax.Precision.HIGHEST
SEQ = ("ctx", "pair")


def split(x):
    high = x.astype(bf16)
    return high, (x - high.astype(f32)).astype(bf16)


def mm(a, b):
    ah, al = split(a)
    bh, bl = split(b)
    lhs = jnp.concatenate([ah, al], axis=1)
    rhs = jnp.concatenate(
        [jnp.concatenate([bh, bl], axis=1), jnp.concatenate([bh, jnp.zeros_like(bh)], axis=1)], axis=0
    )
    r = lax.dot_general(lhs, rhs, (((1,), (0,)), ((), ())), preferred_element_type=f32)
    n = b.shape[1]
    return r[:, :n] + r[:, n:]


def mm_nt(a, b):
    ah, al = split(a)
    bh, bl = split(b)
    lhs = jnp.concatenate([ah, al], axis=1)
    rhs = jnp.concatenate(
        [jnp.concatenate([bh, bh], axis=1), jnp.concatenate([bl, jnp.zeros_like(bl)], axis=1)], axis=0
    )
    r = lax.dot_general(lhs, rhs, (((1,), (1,)), ((), ())), preferred_element_type=f32)
    n = b.shape[0]
    return r[:, :n] + r[:, n:]


def iota(axis):
    return lax.broadcasted_iota(jnp.int32, (CH, CH), axis)


def rowsum(x):
    return jnp.sum(x, axis=1, keepdims=True)


def columns(rows):
    return jnp.concatenate([rows, jnp.zeros((CH - rows.shape[0], CH), f32)], axis=0).T


def sigmoid(a):
    return 1.0 / (1.0 + jnp.exp(-a))


def fetch(raw, recv, flags):
    first = raw[:SWAP, :]
    second = raw[SWAP:, :]
    got = recv[...]
    first = jnp.where(flags[0] > 0, got, first)
    second = jnp.where(flags[1] > 0, got, second)
    return jnp.concatenate([first, second], axis=0)


def conv(x, halo, taps, masks):
    ext = jnp.concatenate([halo, x], axis=0)
    width = x.shape[1] // CH
    total = taps[TAPS - 1 : TAPS, :] * x
    for d in range(1, TAPS):
        moved = pltpu.roll(ext, d, 0)[HALO:, :]
        mask = masks[d - 1]
        if width > 1:
            mask = jnp.concatenate([mask] * width, axis=1)
        total = total + taps[TAPS - 1 - d : TAPS - d, :] * (moved * mask)
    return total


def conv_back(da, taps, masks):
    width = da.shape[1] // CH
    zeros = jnp.zeros((HALO, da.shape[1]), f32)
    total = taps[TAPS - 1 : TAPS, :] * jnp.concatenate([da, zeros], axis=0)
    size = total.shape[0]
    for d in range(1, TAPS):
        mask = masks[d - 1]
        if width > 1:
            mask = jnp.concatenate([mask] * width, axis=1)
        ext = jnp.concatenate([da * mask, zeros], axis=0)
        total = total + taps[TAPS - 1 - d : TAPS - d, :] * pltpu.roll(ext, size - d, 0)
    return total


def local_maps(
    flags, q_raw, k_raw, v_raw, g_raw, q_got, k_got, v_got, g_got, q_halo, k_halo, v_halo,
    q_taps, k_taps, v_taps, masks, docs, rows,
    a_q, a_k, a_v, qn_out, kn_out, seq_grad, inv_out, kk_out, qk_out, pdo_out,
):
    blocks = q_raw.shape[0] // CH
    qa = conv(fetch(q_raw, q_got, flags).astype(f32), q_halo[...], q_taps, masks)
    ka = conv(fetch(k_raw, k_got, flags).astype(f32), k_halo[...], k_taps, masks)
    va = conv(fetch(v_raw, v_got, flags).astype(f32), v_halo[...], v_taps, masks)
    a_q[...] = qa
    a_k[...] = ka
    a_v[...] = va
    gs = fetch(g_raw, g_got, flags)
    seq_grad[...] = gs
    do_all = gs.astype(f32)
    qu = qa * sigmoid(qa)
    ku = ka * sigmoid(ka)
    v_all = va * sigmoid(va)
    qn = qu * (SCALE / jnp.sqrt(rowsum(qu * qu) + GUARD))
    kn = ku * (1.0 / jnp.sqrt(rowsum(ku * ku) + GUARD))
    qn_out[...] = qn
    kn_out[...] = kn
    row, col = iota(0), iota(1)
    eye = (row == col).astype(f32)
    heads = v_raw.shape[1] // CH
    state = []
    for n in range(blocks):
        q = qn[n * CH : (n + 1) * CH]
        k = kn[n * CH : (n + 1) * CH]
        both = mm_nt(jnp.concatenate([k, q], axis=0), k)
        kk, qk = both[:CH], both[CH:]
        kk_out[0, n] = kk
        qk_out[0, n] = qk
        q_t, k_t = q.T, k.T
        flat = rows[0, n]
        cols = columns(flat)
        for e in range(heads):
            beta, c, s, w = [cols[:, 4 * e + i : 4 * e + i + 1] for i in range(4)]
            beta_r, c_r, s_r, w_r = [flat[4 * e + i : 4 * e + i + 1, :] for i in range(4)]
            s_last = s_r[:, CH - 1 :]
            decay = jnp.exp(jnp.minimum(c - c_r, 0.0)) * docs[n]
            low = jnp.where(row > col, beta * decay * kk, 0.0)
            do = do_all[n * CH : (n + 1) * CH, e * CH : (e + 1) * CH]
            v = v_all[n * CH : (n + 1) * CH, e * CH : (e + 1) * CH]
            state.append((n, e, low, decay * qk, do, v, k * w, (beta_r * s_r) * k_t, beta * s * k, s_r * q_t, beta * v, s_last))
    inv = []
    for item in state:
        inv.append(eye - jnp.where((row >> 1) == (col >> 1), item[2], 0.0))
    size = 1
    while (2 << size) <= CH:
        near = ((row >> (size + 1)) == (col >> (size + 1))) & ((row >> size) != (col >> size))
        half = [mm(jnp.where(near, item[2], 0.0), t) for item, t in zip(state, inv)]
        inv = [t - mm(t, h) for t, h in zip(inv, half)]
        size += 1
    maps = {}
    for item, t in zip(state, inv):
        n, e, low, p, do, v, kw, bsk_t, bsk, sq_t, bv, s_last = item
        inv_out[0, e, n] = t
        pdo = mm(p.T, do)
        pdo_out[0, e, n] = pdo
        t_t = t.T
        b = mm(t_t, kw)
        cc = mm(t_t, pdo)
        b_t = b.T
        m = s_last * eye - mm(b_t, bsk)
        a = mm(b_t, bv)
        g = mm(sq_t, do) - mm(bsk_t, cc)
        maps[n, e] = (m, a, g)
    results = []
    for e in range(heads):
        m, a, g = maps[0, e]
        for n in range(1, blocks):
            m2, a2, g2 = maps[n, e]
            g = g + mm(m.T, g2)
            a = mm(m2, a) + a2
            m = mm(m2, m)
        results.append((m, a, g))
    return results


def prepare_kernel(*refs):
    m_out, a_out, g_out = refs[-3:]
    for e, (m, a, g) in enumerate(local_maps(*refs[:-3])):
        m_out[e] = m
        a_out[e] = a
        g_out[e] = g


def exchange_kernel(ctxs, hk, *refs):
    sent, got, kept, kept_map, x_buf, y_buf, y_got, swap_s, swap_r, hop_s, hop_r, pair_s, pair_r = refs[-13:]
    s_out, d_out = refs[-15:-13]
    step = pl.program_id(0)
    core = lax.axis_index("pair")
    ctx = lax.axis_index("ctx")
    first = core == 0
    partner = {"pair": 1 - core}
    peer_ctx = jnp.where(first, ctx - 1, ctx + 1)
    has_peer = (peer_ctx >= 0) & (peer_ctx < ctxs)
    peer = {"ctx": jnp.clip(peer_ctx, 0, ctxs - 1), "pair": 1 - core}
    mesh_id = pl.DeviceIdType.MESH

    def swap(j):
        return pltpu.make_async_remote_copy(
            sent.at[j], got.at[j], swap_s.at[j], swap_r.at[j], device_id=partner, device_id_type=mesh_id
        )

    def hop(j):
        return pltpu.make_async_remote_copy(
            x_buf.at[j], y_buf.at[j], hop_s.at[j], hop_r.at[j], device_id=peer, device_id_type=mesh_id
        )

    def pair(j):
        return pltpu.make_async_remote_copy(
            y_buf.at[j], y_got.at[j], pair_s.at[j], pair_r.at[j], device_id=partner, device_id_type=mesh_id
        )

    @pl.when(step == 0)
    def _():
        barrier = pltpu.get_barrier_semaphore()
        pl.semaphore_signal(barrier, inc=1, device_id=partner, device_id_type=mesh_id)

        @pl.when(has_peer)
        def _():
            pl.semaphore_signal(barrier, inc=1, device_id=peer, device_id_type=mesh_id)

        pl.semaphore_wait(barrier, jnp.where(has_peer, 2, 1))

    @pl.when(step < hk)
    def _():
        for e, (m, a, g) in enumerate(local_maps(*refs[:-15])):
            m_t = m.T
            sent[step, 0, e] = jnp.where(first, a, g)
            sent[step, 1, e] = jnp.where(first, m, m_t)
            kept[step, e] = jnp.where(first, g, a)
            kept_map[step, e] = jnp.where(first, m_t, m)
        swap(step).start()

    @pl.when((step >= 1) & (step < hk + 1))
    def _():
        j = step - 1
        swap(j).wait_recv()
        for e in range(s_out.shape[0]):
            x_buf[j, e] = kept[j, e] + mm(kept_map[j, e], got[j, 0, e])

        @pl.when(has_peer)
        def _():
            hop(j).start()

    @pl.when((step >= 2) & (step < hk + 2))
    def _():
        j = step - 2

        @pl.when(has_peer)
        def _():
            hop(j).wait_recv()

        @pl.when(jnp.logical_not(has_peer))
        def _():
            y_buf[j] = jnp.zeros(y_buf.shape[1:], f32)

        pair(j).start()

    @pl.when(step >= 3)
    def _():
        j = step - 3
        pair(j).wait_recv()
        for e in range(s_out.shape[0]):
            mine = y_buf[j, e]
            other = got[j, 0, e] + mm(got[j, 1, e], y_got[j, e])
            s_out[e] = jnp.where(first, mine, other)
            d_out[e] = jnp.where(first, other, mine)
        swap(j).wait_send()
        pair(j).wait_send()

        @pl.when(has_peer)
        def _():
            hop(j).wait_send()


def join_kernel(m, a, g, a_in, g_in, a_out, g_out):
    for e in range(m.shape[0]):
        here = m[e]
        a_out[e] = a[e] + mm(here, a_in[e])
        g_out[e] = g[e] + mm(here.T, g_in[e])


def norm_back(dy, a, scale):
    sig = sigmoid(a)
    u = a * sig
    inverse = 1.0 / jnp.sqrt(rowsum(u * u) + GUARD)
    y = u * inverse
    dy = dy * scale
    du = (dy - y * rowsum(y * dy)) * inverse
    return du * (sig + u * (1.0 - sig))


def main_kernel(
    a_q, a_k, a_v, qn, kn, seq_grad, inv, kk_in, qk_in, pdo_in, q_taps, k_taps, v_taps, masks, docs, rows,
    s_in, d_in, out, q_grad, k_grad, v_grad, q_end, k_end, v_end, q_spill, k_spill, v_spill, row_grads,
):
    tokens = a_q.shape[0]
    blocks = tokens // CH
    heads = a_v.shape[1] // CH
    row, col = iota(0), iota(1)
    va = a_v[...]
    v_sig = sigmoid(va)
    v_all = va * v_sig
    info = []
    for n in range(blocks):
        q = qn[n * CH : (n + 1) * CH, :]
        k = kn[n * CH : (n + 1) * CH, :]
        info.append((q, k, q.T, k.T, rows[0, n], columns(rows[0, n])))
    fwd = {}
    carried = [s_in[e] for e in range(heads)]
    for n in range(blocks):
        q, k, q_t, k_t, flat, cols = info[n]
        kq = jnp.concatenate([k, q], axis=0)
        for e in range(heads):
            beta, c, s, w = [cols[:, 4 * e + i : 4 * e + i + 1] for i in range(4)]
            beta_r, c_r, s_r, w_r = [flat[4 * e + i : 4 * e + i + 1, :] for i in range(4)]
            s_last = s_r[:, CH - 1 :]
            v = v_all[n * CH : (n + 1) * CH, e * CH : (e + 1) * CH]
            decay = jnp.exp(jnp.minimum(c - c_r, 0.0)) * docs[n]
            p = decay * qk_in[0, n]
            st = carried[e]
            kqs = mm(kq, st)
            ks, qs = kqs[:CH], kqs[CH:]
            t = inv[0, e, n]
            u = mm(t, beta * (v - s * ks))
            o = s * qs + mm(p, u)
            out[n * CH : (n + 1) * CH, e * CH : (e + 1) * CH] = o.astype(bf16)
            if n + 1 < blocks:
                carried[e] = s_last * st + mm(k_t * w_r, u)
            fwd[n, e] = (st, u, qs, decay, p, v)
    grads = [d_in[e] for e in range(heads)]
    dqs, dks, dvs = [None] * blocks, [None] * blocks, {}
    for n in reversed(range(blocks)):
        q, k, q_t, k_t, flat, cols = info[n]
        packed = jnp.zeros((CH, CH), f32)
        dqk_sum = dkk_sum = dq = dk = 0.0
        for e in range(heads):
            beta, c, s, w = [cols[:, 4 * e + i : 4 * e + i + 1] for i in range(4)]
            beta_r, c_r, s_r, w_r = [flat[4 * e + i : 4 * e + i + 1, :] for i in range(4)]
            s_last = s_r[:, CH - 1 :]
            st, u, qs, decay, p, v = fwd[n, e]
            ds_out = grads[e]
            do = seq_grad[n * CH : (n + 1) * CH, e * CH : (e + 1) * CH].astype(f32)
            du = pdo_in[0, e, n] + mm(k * w, ds_out)
            y = mm(inv[0, e, n].T, du)
            do_y = jnp.concatenate([do, y], axis=0)
            by_u = mm_nt(do_y, u)
            by_s = mm_nt(do_y, st)
            dp, dl = by_u[:CH], -by_u[CH:]
            dos, z = by_s[:CH], -by_s[CH:]
            dkw = mm_nt(u, ds_out)
            strict = jnp.where(row > col, decay, 0.0)
            bk = strict * kk_in[0, n]
            dlb = dl * bk
            f = dp * p + beta * dlb
            zk = z * k
            wk = w * (dkw * k)
            bs = beta * s
            dbeta = rowsum(y * v + s * zk + dlb)
            extra = jnp.sum(rowsum(wk + s_last * (ds_out * st)), axis=0, keepdims=True)
            dc = rowsum((f - f.T) + s * (do * qs) + bs * zk - wk)
            dc = dc + jnp.where(row[:, :1] == CH - 1, extra, 0.0)
            packed = jnp.where(col == 2 * e, dbeta, packed)
            packed = jnp.where(col == 2 * e + 1, dc, packed)
            dqk_sum = dqk_sum + dp * decay
            dkk_sum = dkk_sum + dl * (beta * strict)
            dq = dq + s * dos
            dk = dk + w * dkw + bs * z
            dvs[n, e] = beta * y
            if n > 0:
                grads[e] = mm(q_t * s_r, do) + s_last * ds_out - mm(k_t * (beta_r * s_r), y)
        dqs[n] = dq + mm(dqk_sum, k)
        dks[n] = dk + mm(dqk_sum.T, q) + mm(dkk_sum + dkk_sum.T, k)
        row_grads[0, n] = packed.T[: row_grads.shape[2]]
    dq = jnp.concatenate(dqs, axis=0)
    dk = jnp.concatenate(dks, axis=0)
    dv = jnp.concatenate(
        [jnp.concatenate([dvs[n, e] for e in range(heads)], axis=1) for n in range(blocks)], axis=0
    )
    daq = norm_back(dq, a_q[...], SCALE)
    dak = norm_back(dk, a_k[...], 1.0)
    dav = dv * (v_sig + v_all * (1.0 - v_sig))
    for da, taps, grad, end, spill in (
        (daq, q_taps, q_grad, q_end, q_spill),
        (dak, k_taps, k_grad, k_end, k_spill),
        (dav, v_taps, v_grad, v_end, v_spill),
    ):
        full = conv_back(da, taps, masks)
        grad[...] = full[:tokens].astype(bf16)
        end[...] = full[tokens - HALO : tokens]
        spill[...] = full[tokens:]


def shifted(array, by):
    peers = lax.axis_size(SEQ)
    return lax.ppermute(array, SEQ, [(i, i + by) for i in range(peers) if 0 <= i + by < peers])


def tri(upper):
    i = jnp.arange(CH)
    return ((i[:, None] <= i[None, :]) if upper else (i[:, None] >= i[None, :])).astype(f32)


def sds(shape, dtype=f32):
    return jax.ShapeDtypeStruct(shape, dtype)


def body(
    q_raw, k_raw, v_raw, beta_logit, gate_logit, out_grad, conv_q, conv_k, conv_v, a_log, dt_bias, doc_ids, swap_blocks
):
    tokens = q_raw.shape[0]
    blocks = tokens // CH
    hk = q_raw.shape[1] // DK
    hv = v_raw.shape[1] // DK
    rep = hv // hk
    shards = lax.axis_size(SEQ)
    hops = max(1, shards // DOC_PARTS)
    core = lax.axis_index("pair")
    swap = swap_blocks[0]
    flags = jnp.stack([jnp.where(core == 1, swap, 0), jnp.where(core == 0, swap, 0)]).astype(jnp.int32)

    start = jnp.where(core == 0, SWAP, 0)
    logits = jnp.concatenate([beta_logit, gate_logit], axis=0)
    bg_send = lax.dynamic_slice_in_dim(logits, start, SWAP, 1)
    send = jnp.concatenate(
        [lax.dynamic_slice_in_dim(x, start, SWAP, 0) for x in (q_raw, k_raw, v_raw, out_grad)], axis=1
    )
    got, bg_got = lax.ppermute((send, bg_send), "pair", [(0, 1), (1, 0)])
    ids_col = jnp.broadcast_to((doc_ids[tokens - HALO :] + 1).astype(bf16)[:, None], (HALO, CH))
    tail = jnp.concatenate([x[tokens - HALO :] for x in (q_raw, k_raw, v_raw)] + [ids_col], axis=1)
    before = shifted(tail, 1)
    own = jnp.concatenate([x[SWAP - HALO : SWAP] for x in (q_raw, k_raw, v_raw)], axis=1)
    chans = own.shape[1]
    halo = jnp.where(flags[0] > 0, own, before[:, :chans]).astype(f32)
    qw = hk * DK

    first = jnp.where(flags[0] > 0, bg_got, logits[:, :SWAP])
    second = jnp.where(flags[1] > 0, bg_got, logits[:, SWAP:])
    logits = jnp.concatenate([first, second], axis=1).astype(f32)
    beta = jax.nn.sigmoid(logits[:hv])
    gate = logits[hv:] + dt_bias[:, None]
    rate = -jnp.exp(a_log)[:, None]
    decay_log = rate * jax.nn.softplus(gate)
    c = jnp.dot(decay_log.reshape(hv * blocks, CH), tri(True), precision=highest).reshape(hv, blocks, CH)
    ids = doc_ids.astype(f32) + 1.0
    ext_ids = jnp.concatenate([before[:, chans].astype(f32), ids])
    doc = ids.reshape(blocks, CH)
    doc_before = ext_ids[HALO - 1 : HALO - 1 + tokens : CH]
    s = jnp.where(doc == doc_before[:, None], jnp.exp(c), 0.0)
    w = jnp.where(doc == doc[:, CH - 1 :], jnp.exp(jnp.minimum(c[:, :, CH - 1 :] - c, 0.0)), 0.0)
    rows = jnp.stack([beta.reshape(hv, blocks, CH), c, s, w], axis=2)
    rows = rows.reshape(hk, rep, blocks, 4, CH).transpose(0, 2, 1, 3, 4).reshape(hk, blocks, rep * 4, CH)
    docs = ((doc[:, :, None] == doc[:, None, :]) & (tri(False) > 0)[None]).astype(f32)
    masks = jnp.stack(
        [
            jnp.broadcast_to((ext_ids[HALO - d : HALO - d + tokens] == ids).astype(f32)[:, None], (tokens, CH))
            for d in range(1, TAPS)
        ]
    )
    taps = [x.astype(f32) for x in (conv_q, conv_k, conv_v)]

    vw = rep * DK
    col = lambda rows_, width, off=0: pl.BlockSpec((rows_, width), lambda i, off=off, width=width: (0, off // width + i))
    fixed = lambda shape: pl.BlockSpec(shape, lambda i: (0,) * len(shape))
    per = lambda shape: pl.BlockSpec(shape, lambda i: (i,) + (0,) * (len(shape) - 1))
    taps_specs = [col(TAPS, DK), col(TAPS, DK), col(TAPS, vw)]
    common_specs = taps_specs + [
        fixed((TAPS - 1, tokens, CH)),
        fixed((blocks, CH, CH)),
        per((1, blocks, rep * 4, CH)),
    ]
    params = pltpu.CompilerParams(dimension_semantics=("arbitrary",), vmem_limit_bytes=48 * 2**20)
    saved_specs = [
        col(tokens, DK), col(tokens, DK), col(tokens, vw), col(tokens, DK), col(tokens, DK), col(tokens, vw),
        per((1, rep, blocks, CH, CH)), per((1, blocks, CH, CH)), per((1, blocks, CH, CH)),
        per((1, rep, blocks, CH, CH)),
    ]
    saved_shapes = [
        sds((tokens, qw)), sds((tokens, qw)), sds((tokens, hv * DK)), sds((tokens, qw)), sds((tokens, qw)),
        sds((tokens, hv * DK), bf16), sds((hk, rep, blocks, CH, CH)), sds((hk, blocks, CH, CH)),
        sds((hk, blocks, CH, CH)), sds((hk, rep, blocks, CH, CH)),
    ]
    state_spec = per((rep, DK, DK))
    state_shape = sds((hv, DK, DK))
    units = hv * blocks * 2 * 4 * CH**3
    inputs = (flags, q_raw, k_raw, v_raw, out_grad, got, got, got, got, halo, halo, halo, *taps, masks, docs, rows)
    in_specs = [
        pl.BlockSpec(memory_space=pltpu.SMEM),
        col(tokens, DK), col(tokens, DK), col(tokens, vw), col(tokens, vw),
        col(SWAP, DK), col(SWAP, DK, qw), col(SWAP, vw, 2 * qw), col(SWAP, vw, 2 * qw + hv * DK),
        col(HALO, DK), col(HALO, DK, qw), col(HALO, vw, 2 * qw),
    ] + common_specs
    prepare_cost = pl.CostEstimate(flops=22 * units, bytes_accessed=24 * 2**20, transcendentals=2**20)
    if shards // DOC_PARTS == lax.axis_size("pair"):

        def held(spec, lag):
            if spec.index_map is None:
                return spec
            index = spec.index_map
            return pl.BlockSpec(spec.block_shape, lambda i: index(jnp.clip(i - lag, 0, hk - 1)))

        sems = pltpu.SemaphoreType.DMA((hk,))
        states = pltpu.VMEM((hk, rep, DK, DK), f32)
        prepared = pl.pallas_call(
            functools.partial(exchange_kernel, lax.axis_size("ctx"), hk),
            grid=(hk + 3,),
            in_specs=[held(spec, 0) for spec in in_specs],
            out_specs=[held(spec, 0) for spec in saved_specs] + [held(state_spec, 3)] * 2,
            out_shape=saved_shapes + [state_shape] * 2,
            scratch_shapes=[pltpu.VMEM((hk, 2, rep, DK, DK), f32)] * 2 + [states] * 5 + [sems] * 6,
            compiler_params=pltpu.CompilerParams(
                dimension_semantics=("arbitrary",), vmem_limit_bytes=48 * 2**20, collective_id=0,
                has_side_effects=True,
            ),
            cost_estimate=prepare_cost,
            name="exchange",
        )(*inputs)
        saved, (s_in, d_in) = prepared[:10], prepared[10:]
    else:
        prepared = pl.pallas_call(
            prepare_kernel,
            grid=(hk,),
            in_specs=in_specs,
            out_specs=saved_specs + [state_spec] * 3,
            out_shape=saved_shapes + [state_shape] * 3,
            compiler_params=params,
            cost_estimate=prepare_cost,
            name="prepare",
        )(*inputs)
        saved, (m, a, g) = prepared[:10], prepared[10:]
        join = pl.pallas_call(
            join_kernel,
            grid=(hk,),
            in_specs=[state_spec] * 5,
            out_specs=[state_spec] * 2,
            out_shape=[state_shape] * 2,
            compiler_params=params,
            cost_estimate=pl.CostEstimate(flops=hv * 16 * CH**3, bytes_accessed=7 * 2**20, transcendentals=0),
            name="join",
        )
        s_in, d_in = a, g
        for step in range(hops):
            s_in, d_in = shifted(s_in, 1), shifted(d_in, -1)
            if step < hops - 1:
                s_in, d_in = join(m, a, g, s_in, d_in)

    ends = [col(HALO, DK), col(HALO, DK), col(HALO, vw)]
    end_shapes = [sds((HALO, qw)), sds((HALO, qw)), sds((HALO, hv * DK))]
    results = pl.pallas_call(
        main_kernel,
        grid=(hk,),
        in_specs=saved_specs + common_specs + [state_spec] * 2,
        out_specs=[col(tokens, vw), col(tokens, DK), col(tokens, DK), col(tokens, vw)] + ends + ends + [per((1, blocks, 8, CH))],
        out_shape=[
            sds((tokens, hv * DK), bf16), sds((tokens, qw), bf16), sds((tokens, qw), bf16), sds((tokens, hv * DK), bf16)
        ] + end_shapes + end_shapes + [sds((hk, blocks, 8, CH))],
        compiler_params=params,
        cost_estimate=pl.CostEstimate(flops=17 * units, bytes_accessed=24 * 2**20, transcendentals=2**20),
        name="main",
    )(*saved, *taps, masks, docs, rows, s_in, d_in)
    layer_out, q_grad, k_grad, v_grad = results[:4]
    spilled = shifted(jnp.concatenate(results[7:10], axis=1), -1)
    ends_out = []
    at = 0
    for grad, end in zip((q_grad, k_grad, v_grad), results[4:7]):
        width = end.shape[1]
        last = (end + spilled[:, at : at + width]).astype(bf16)
        ends_out.append(lax.dynamic_update_slice(grad, last, (tokens - HALO, 0)))
        at += width
    rg = results[10][:, :, : 2 * rep].reshape(hk, blocks, rep, 2, CH).transpose(3, 0, 2, 1, 4)
    dbeta = rg[0].reshape(hv, tokens)
    dg = jnp.dot(rg[1].reshape(hv * blocks, CH), tri(False), precision=highest).reshape(hv, tokens)
    beta_grad = dbeta * beta * (1.0 - beta)
    gate_grad = dg * rate * jax.nn.sigmoid(gate)
    return (layer_out, ends_out[0], ends_out[1], ends_out[2], beta_grad.astype(bf16), gate_grad.astype(bf16))


def solution(mesh):
    rows = P(("groups", "ctx", "pair"), "head")
    rates = P("head", ("groups", "ctx", "pair"))
    taps = P(None, "head")
    return jax.shard_map(
        body,
        mesh=mesh,
        in_specs=(
            rows, rows, rows, rates, rates, rows, taps, taps, taps, P("head"), P("head"),
            P(("groups", "ctx", "pair")), P(("groups", "ctx")),
        ),
        out_specs=(rows, rows, rows, rows, rates, rates),
        check_vma=False,
    )
```

```python
import functools
import math

import jax
import jax.numpy as jnp
from jax import lax
from jax.experimental import pallas as pl
from jax.experimental.pallas import tpu as pltpu
from jax.sharding import PartitionSpec as P

DK = 128
TAPS = 4
CH = 128
SWAP = 128
HALO = 8
GUARD = 1e-06
SCALE = 1.0 / math.sqrt(DK)
DOC_PARTS = 4

f32 = jnp.float32
bf16 = jnp.bfloat16
highest = lax.Precision.HIGHEST
SEQ = ("ctx", "pair")


def split(x):
    high = x.astype(bf16)
    return high, (x - high.astype(f32)).astype(bf16)


def mm(a, b):
    ah, al = split(a)
    bh, bl = split(b)
    lhs = jnp.concatenate([ah, al], axis=1)
    rhs = jnp.concatenate(
        [jnp.concatenate([bh, bl], axis=1), jnp.concatenate([bh, jnp.zeros_like(bh)], axis=1)], axis=0
    )
    r = lax.dot_general(lhs, rhs, (((1,), (0,)), ((), ())), preferred_element_type=f32)
    n = b.shape[1]
    return r[:, :n] + r[:, n:]


def mm_half(a, b):
    return lax.dot_general(
        jnp.concatenate(split(a), axis=1), jnp.concatenate([b, b], axis=0), (((1,), (0,)), ((), ())),
        preferred_element_type=f32,
    )


def odd_blocks(x, size):
    return jnp.concatenate([x[i : i + size] for i in range(size, CH, 2 * size)], axis=0)


def with_odd(even, odd, size):
    parts = []
    for i in range(0, CH // 2, size):
        parts.append(jnp.zeros((size, CH), odd.dtype) if even is None else even[2 * i : 2 * i + size])
        parts.append(odd[i : i + size])
    return jnp.concatenate(parts, axis=0)


def mm_nt(a, b):
    ah, al = split(a)
    bh, bl = split(b)
    lhs = jnp.concatenate([ah, al], axis=1)
    rhs = jnp.concatenate(
        [jnp.concatenate([bh, bh], axis=1), jnp.concatenate([bl, jnp.zeros_like(bl)], axis=1)], axis=0
    )
    r = lax.dot_general(lhs, rhs, (((1,), (1,)), ((), ())), preferred_element_type=f32)
    n = b.shape[0]
    return r[:, :n] + r[:, n:]


def iota(axis):
    return lax.broadcasted_iota(jnp.int32, (CH, CH), axis)


def rowsum(x):
    return jnp.sum(x, axis=1, keepdims=True)


def columns(rows):
    return jnp.concatenate([rows, jnp.zeros((CH - rows.shape[0], CH), f32)], axis=0).T


def sigmoid(a):
    return 1.0 / (1.0 + jnp.exp(-a))


def fetch(raw, recv, flags):
    first = raw[:SWAP, :]
    second = raw[SWAP:, :]
    got = recv[...]
    first = jnp.where(flags[0] > 0, got, first)
    second = jnp.where(flags[1] > 0, got, second)
    return jnp.concatenate([first, second], axis=0)


def conv(x, halo, taps, masks):
    ext = jnp.concatenate([halo, x], axis=0)
    width = x.shape[1] // CH
    total = taps[TAPS - 1 : TAPS, :] * x
    for d in range(1, TAPS):
        moved = pltpu.roll(ext, d, 0)[HALO:, :]
        mask = masks[d - 1]
        if width > 1:
            mask = jnp.concatenate([mask] * width, axis=1)
        total = total + taps[TAPS - 1 - d : TAPS - d, :] * (moved * mask)
    return total


def conv_back(da, taps, masks):
    width = da.shape[1] // CH
    zeros = jnp.zeros((HALO, da.shape[1]), f32)
    total = taps[TAPS - 1 : TAPS, :] * jnp.concatenate([da, zeros], axis=0)
    size = total.shape[0]
    for d in range(1, TAPS):
        mask = masks[d - 1]
        if width > 1:
            mask = jnp.concatenate([mask] * width, axis=1)
        ext = jnp.concatenate([da * mask, zeros], axis=0)
        total = total + taps[TAPS - 1 - d : TAPS - d, :] * pltpu.roll(ext, size - d, 0)
    return total


def local_maps(
    flags, q_raw, k_raw, v_raw, g_raw, q_got, k_got, v_got, g_got, q_halo, k_halo, v_halo,
    q_taps, k_taps, v_taps, masks, docs, rows,
    a_q, a_k, a_v, qn_out, kn_out, seq_grad, inv_out, kk_out, qk_out, pdo_out,
):
    blocks = q_raw.shape[0] // CH
    qa = conv(fetch(q_raw, q_got, flags).astype(f32), q_halo[...], q_taps, masks)
    ka = conv(fetch(k_raw, k_got, flags).astype(f32), k_halo[...], k_taps, masks)
    va = conv(fetch(v_raw, v_got, flags).astype(f32), v_halo[...], v_taps, masks)
    a_q[...] = qa
    a_k[...] = ka
    a_v[...] = va
    gs = fetch(g_raw, g_got, flags)
    seq_grad[...] = gs
    do_all = gs
    qu = qa * sigmoid(qa)
    ku = ka * sigmoid(ka)
    v_all = va * sigmoid(va)
    qn = qu * (SCALE / jnp.sqrt(rowsum(qu * qu) + GUARD))
    kn = ku * (1.0 / jnp.sqrt(rowsum(ku * ku) + GUARD))
    qn_out[...] = qn
    kn_out[...] = kn
    row, col = iota(0), iota(1)
    eye = (row == col).astype(f32)
    heads = v_raw.shape[1] // CH
    state = []
    for n in range(blocks):
        q = qn[n * CH : (n + 1) * CH]
        k = kn[n * CH : (n + 1) * CH]
        both = mm_nt(jnp.concatenate([k, q], axis=0), k)
        kk, qk = both[:CH], both[CH:]
        kk_out[0, n] = kk
        qk_out[0, n] = qk
        q_t, k_t = q.T, k.T
        flat = rows[0, n]
        cols = columns(flat)
        for e in range(heads):
            beta, c, s, w = [cols[:, 4 * e + i : 4 * e + i + 1] for i in range(4)]
            beta_r, c_r, s_r, w_r = [flat[4 * e + i : 4 * e + i + 1, :] for i in range(4)]
            s_last = s_r[:, CH - 1 :]
            decay = jnp.exp(jnp.minimum(c - c_r, 0.0)) * docs[n]
            low = jnp.where(row > col, beta * decay * kk, 0.0)
            do = do_all[n * CH : (n + 1) * CH, e * CH : (e + 1) * CH]
            v = v_all[n * CH : (n + 1) * CH, e * CH : (e + 1) * CH]
            state.append((n, e, low, decay * qk, do, v, k * w, (beta_r * s_r) * k_t, beta * s * k, s_r * q_t, beta * v, s_last))
    inv = []
    for item in state:
        inv.append(eye - jnp.where((row >> 1) == (col >> 1), item[2], 0.0))
    size = 1
    while (2 << size) <= CH:
        near = ((row >> (size + 1)) == (col >> (size + 1))) & ((row >> size) != (col >> size))
        width = 1 << size
        if width < 8:
            half = [mm(jnp.where(near, item[2], 0.0), t) for item, t in zip(state, inv)]
            inv = [t - mm(t, h) for t, h in zip(inv, half)]
        else:
            half = [mm(odd_blocks(jnp.where(near, item[2], 0.0), width), t) for item, t in zip(state, inv)]
            odds = [odd_blocks(t, width) for t in inv]
            odds = [t - mm(t, with_odd(None, h, width)) for t, h in zip(odds, half)]
            inv = [with_odd(t, o, width) for t, o in zip(inv, odds)]
        size += 1
    maps = {}
    for item, t in zip(state, inv):
        n, e, low, p, do, v, kw, bsk_t, bsk, sq_t, bv, s_last = item
        inv_out[0, e, n] = t
        pdo = mm_half(p.T, do)
        pdo_out[0, e, n] = pdo
        t_t = t.T
        b = mm(t_t, kw)
        cc = mm(t_t, pdo)
        b_t = b.T
        m = s_last * eye - mm(b_t, bsk)
        a = mm(b_t, bv)
        g = mm_half(sq_t, do) - mm(bsk_t, cc)
        maps[n, e] = (m, a, g)
    results = []
    for e in range(heads):
        m, a, g = maps[0, e]
        for n in range(1, blocks):
            m2, a2, g2 = maps[n, e]
            g = g + mm(m.T, g2)
            a = mm(m2, a) + a2
            m = mm(m2, m)
        results.append((m, a, g))
    return results


def prepare_kernel(*refs):
    m_out, a_out, g_out = refs[-3:]
    for e, (m, a, g) in enumerate(local_maps(*refs[:-3])):
        m_out[e] = m
        a_out[e] = a
        g_out[e] = g


def exchange_kernel(ctxs, hk, *refs):
    sent, got, kept, kept_map, x_buf, y_buf, y_got, swap_s, swap_r, hop_s, hop_r, pair_s, pair_r = refs[-13:]
    s_out, d_out = refs[-15:-13]
    step = pl.program_id(0)
    core = lax.axis_index("pair")
    ctx = lax.axis_index("ctx")
    first = core == 0
    partner = {"pair": 1 - core}
    peer_ctx = jnp.where(first, ctx - 1, ctx + 1)
    has_peer = (peer_ctx >= 0) & (peer_ctx < ctxs)
    peer = {"ctx": jnp.clip(peer_ctx, 0, ctxs - 1), "pair": 1 - core}
    mesh_id = pl.DeviceIdType.MESH

    def swap(j):
        return pltpu.make_async_remote_copy(
            sent.at[j], got.at[j], swap_s.at[j], swap_r.at[j], device_id=partner, device_id_type=mesh_id
        )

    def hop(j):
        return pltpu.make_async_remote_copy(
            x_buf.at[j], y_buf.at[j], hop_s.at[j], hop_r.at[j], device_id=peer, device_id_type=mesh_id
        )

    def pair(j):
        return pltpu.make_async_remote_copy(
            y_buf.at[j], y_got.at[j], pair_s.at[j], pair_r.at[j], device_id=partner, device_id_type=mesh_id
        )

    @pl.when(step == 0)
    def _():
        barrier = pltpu.get_barrier_semaphore()
        pl.semaphore_signal(barrier, inc=1, device_id=partner, device_id_type=mesh_id)

        @pl.when(has_peer)
        def _():
            pl.semaphore_signal(barrier, inc=1, device_id=peer, device_id_type=mesh_id)

        pl.semaphore_wait(barrier, jnp.where(has_peer, 2, 1))

    @pl.when(step < hk)
    def _():
        for e, (m, a, g) in enumerate(local_maps(*refs[:-15])):
            m_t = m.T
            sent[step, 0, e] = jnp.where(first, a, g)
            sent[step, 1, e] = jnp.where(first, m, m_t)
            kept[step, e] = jnp.where(first, g, a)
            kept_map[step, e] = jnp.where(first, m_t, m)
        swap(step).start()

    @pl.when((step >= 1) & (step < hk + 1))
    def _():
        j = step - 1
        swap(j).wait_recv()
        for e in range(s_out.shape[0]):
            x_buf[j, e] = kept[j, e] + mm(kept_map[j, e], got[j, 0, e])

        @pl.when(has_peer)
        def _():
            hop(j).start()

    @pl.when((step >= 2) & (step < hk + 2))
    def _():
        j = step - 2

        @pl.when(has_peer)
        def _():
            hop(j).wait_recv()

        @pl.when(jnp.logical_not(has_peer))
        def _():
            y_buf[j] = jnp.zeros(y_buf.shape[1:], f32)

        pair(j).start()

    @pl.when(step >= 3)
    def _():
        j = step - 3
        pair(j).wait_recv()
        for e in range(s_out.shape[0]):
            mine = y_buf[j, e]
            other = got[j, 0, e] + mm(got[j, 1, e], y_got[j, e])
            s_out[e] = jnp.where(first, mine, other)
            d_out[e] = jnp.where(first, other, mine)
        swap(j).wait_send()
        pair(j).wait_send()

        @pl.when(has_peer)
        def _():
            hop(j).wait_send()


def join_kernel(m, a, g, a_in, g_in, a_out, g_out):
    for e in range(m.shape[0]):
        here = m[e]
        a_out[e] = a[e] + mm(here, a_in[e])
        g_out[e] = g[e] + mm(here.T, g_in[e])


def norm_back(dy, a, scale):
    sig = sigmoid(a)
    u = a * sig
    inverse = 1.0 / jnp.sqrt(rowsum(u * u) + GUARD)
    y = u * inverse
    dy = dy * scale
    du = (dy - y * rowsum(y * dy)) * inverse
    return du * (sig + u * (1.0 - sig))


def main_kernel(
    a_q, a_k, a_v, qn, kn, seq_grad, inv, kk_in, qk_in, pdo_in, q_taps, k_taps, v_taps, masks, docs, rows,
    s_in, d_in, out, q_grad, k_grad, v_grad, q_end, k_end, v_end, q_spill, k_spill, v_spill, row_grads,
):
    tokens = a_q.shape[0]
    blocks = tokens // CH
    heads = a_v.shape[1] // CH
    row, col = iota(0), iota(1)
    va = a_v[...]
    v_sig = sigmoid(va)
    v_all = va * v_sig
    info = []
    for n in range(blocks):
        q = qn[n * CH : (n + 1) * CH, :]
        k = kn[n * CH : (n + 1) * CH, :]
        info.append((q, k, q.T, k.T, rows[0, n], columns(rows[0, n])))
    fwd = {}
    carried = [s_in[e] for e in range(heads)]
    for n in range(blocks):
        q, k, q_t, k_t, flat, cols = info[n]
        kq = jnp.concatenate([k, q], axis=0)
        for e in range(heads):
            beta, c, s, w = [cols[:, 4 * e + i : 4 * e + i + 1] for i in range(4)]
            beta_r, c_r, s_r, w_r = [flat[4 * e + i : 4 * e + i + 1, :] for i in range(4)]
            s_last = s_r[:, CH - 1 :]
            v = v_all[n * CH : (n + 1) * CH, e * CH : (e + 1) * CH]
            decay = jnp.exp(jnp.minimum(c - c_r, 0.0)) * docs[n]
            p = decay * qk_in[0, n]
            st = carried[e]
            kqs = mm(kq, st)
            ks, qs = kqs[:CH], kqs[CH:]
            t = inv[0, e, n]
            u = mm(t, beta * (v - s * ks))
            o = s * qs + mm(p, u)
            out[n * CH : (n + 1) * CH, e * CH : (e + 1) * CH] = o.astype(bf16)
            if n + 1 < blocks:
                carried[e] = s_last * st + mm(k_t * w_r, u)
            fwd[n, e] = (st, u, qs, decay, p, v)
    grads = [d_in[e] for e in range(heads)]
    dqs, dks, dvs = [None] * blocks, [None] * blocks, {}
    for n in reversed(range(blocks)):
        q, k, q_t, k_t, flat, cols = info[n]
        packed = jnp.zeros((CH, CH), f32)
        dqk_sum = dkk_sum = dq = dk = 0.0
        for e in range(heads):
            beta, c, s, w = [cols[:, 4 * e + i : 4 * e + i + 1] for i in range(4)]
            beta_r, c_r, s_r, w_r = [flat[4 * e + i : 4 * e + i + 1, :] for i in range(4)]
            s_last = s_r[:, CH - 1 :]
            st, u, qs, decay, p, v = fwd[n, e]
            ds_out = grads[e]
            do_half = seq_grad[n * CH : (n + 1) * CH, e * CH : (e + 1) * CH]
            do = do_half.astype(f32)
            du = pdo_in[0, e, n] + mm(k * w, ds_out)
            y = mm(inv[0, e, n].T, du)
            do_y = jnp.concatenate([do, y], axis=0)
            by_u = mm_nt(do_y, u)
            by_s = mm_nt(do_y, st)
            dp, dl = by_u[:CH], -by_u[CH:]
            dos, z = by_s[:CH], -by_s[CH:]
            dkw = mm_nt(u, ds_out)
            strict = jnp.where(row > col, decay, 0.0)
            bk = strict * kk_in[0, n]
            dlb = dl * bk
            f = dp * p + beta * dlb
            zk = z * k
            wk = w * (dkw * k)
            bs = beta * s
            dbeta = rowsum(y * v + s * zk + dlb)
            extra = jnp.sum(rowsum(wk + s_last * (ds_out * st)), axis=0, keepdims=True)
            dc = rowsum((f - f.T) + s * (do * qs) + bs * zk - wk)
            dc = dc + jnp.where(row[:, :1] == CH - 1, extra, 0.0)
            packed = jnp.where(col == 2 * e, dbeta, packed)
            packed = jnp.where(col == 2 * e + 1, dc, packed)
            dqk_sum = dqk_sum + dp * decay
            dkk_sum = dkk_sum + dl * (beta * strict)
            dq = dq + s * dos
            dk = dk + w * dkw + bs * z
            dvs[n, e] = beta * y
            if n > 0:
                grads[e] = mm_half(q_t * s_r, do_half) + s_last * ds_out - mm(k_t * (beta_r * s_r), y)
        dqs[n] = dq + mm(dqk_sum, k)
        dks[n] = dk + mm(dqk_sum.T, q) + mm(dkk_sum + dkk_sum.T, k)
        row_grads[0, n] = packed.T[: row_grads.shape[2]]
    dq = jnp.concatenate(dqs, axis=0)
    dk = jnp.concatenate(dks, axis=0)
    dv = jnp.concatenate(
        [jnp.concatenate([dvs[n, e] for e in range(heads)], axis=1) for n in range(blocks)], axis=0
    )
    daq = norm_back(dq, a_q[...], SCALE)
    dak = norm_back(dk, a_k[...], 1.0)
    dav = dv * (v_sig + v_all * (1.0 - v_sig))
    for da, taps, grad, end, spill in (
        (daq, q_taps, q_grad, q_end, q_spill),
        (dak, k_taps, k_grad, k_end, k_spill),
        (dav, v_taps, v_grad, v_end, v_spill),
    ):
        full = conv_back(da, taps, masks)
        grad[...] = full[:tokens].astype(bf16)
        end[...] = full[tokens - HALO : tokens]
        spill[...] = full[tokens:]


def shifted(array, by):
    peers = lax.axis_size(SEQ)
    return lax.ppermute(array, SEQ, [(i, i + by) for i in range(peers) if 0 <= i + by < peers])


def tri(upper):
    i = jnp.arange(CH)
    return ((i[:, None] <= i[None, :]) if upper else (i[:, None] >= i[None, :])).astype(f32)


def sds(shape, dtype=f32):
    return jax.ShapeDtypeStruct(shape, dtype)


def body(
    q_raw, k_raw, v_raw, beta_logit, gate_logit, out_grad, conv_q, conv_k, conv_v, a_log, dt_bias, doc_ids, swap_blocks
):
    tokens = q_raw.shape[0]
    blocks = tokens // CH
    hk = q_raw.shape[1] // DK
    hv = v_raw.shape[1] // DK
    rep = hv // hk
    shards = lax.axis_size(SEQ)
    hops = max(1, shards // DOC_PARTS)
    core = lax.axis_index("pair")
    swap = swap_blocks[0]
    flags = jnp.stack([jnp.where(core == 1, swap, 0), jnp.where(core == 0, swap, 0)]).astype(jnp.int32)

    start = jnp.where(core == 0, SWAP, 0)
    logits = jnp.concatenate([beta_logit, gate_logit], axis=0)
    bg_send = lax.dynamic_slice_in_dim(logits, start, SWAP, 1)
    send = jnp.concatenate(
        [lax.dynamic_slice_in_dim(x, start, SWAP, 0) for x in (q_raw, k_raw, v_raw, out_grad)], axis=1
    )
    got = lax.ppermute(send, "pair", [(0, 1), (1, 0)])
    send, bg_send, tail_ids, tails = lax.optimization_barrier(
        (send, bg_send, doc_ids[tokens - HALO :], [x[tokens - HALO :] for x in (q_raw, k_raw, v_raw)])
    )
    bg_got = lax.ppermute(bg_send, "pair", [(0, 1), (1, 0)])
    ids_col = jnp.broadcast_to((tail_ids + 1).astype(bf16)[:, None], (HALO, CH))
    tail = jnp.concatenate(tails + [ids_col], axis=1)
    before = shifted(tail, 1)
    own = jnp.concatenate([x[SWAP - HALO : SWAP] for x in (q_raw, k_raw, v_raw)], axis=1)
    chans = own.shape[1]
    halo = jnp.where(flags[0] > 0, own, before[:, :chans]).astype(f32)
    qw = hk * DK

    first = jnp.where(flags[0] > 0, bg_got, logits[:, :SWAP])
    second = jnp.where(flags[1] > 0, bg_got, logits[:, SWAP:])
    logits = jnp.concatenate([first, second], axis=1).astype(f32)
    beta = jax.nn.sigmoid(logits[:hv])
    gate = logits[hv:] + dt_bias[:, None]
    rate = -jnp.exp(a_log)[:, None]
    decay_log = rate * jax.nn.softplus(gate)
    c = jnp.dot(decay_log.reshape(hv * blocks, CH), tri(True), precision=highest).reshape(hv, blocks, CH)
    ids = doc_ids.astype(f32) + 1.0
    ext_ids = jnp.concatenate([before[:, chans].astype(f32), ids])
    doc = ids.reshape(blocks, CH)
    doc_before = ext_ids[HALO - 1 : HALO - 1 + tokens : CH]
    s = jnp.where(doc == doc_before[:, None], jnp.exp(c), 0.0)
    w = jnp.where(doc == doc[:, CH - 1 :], jnp.exp(jnp.minimum(c[:, :, CH - 1 :] - c, 0.0)), 0.0)
    rows = jnp.stack([beta.reshape(hv, blocks, CH), c, s, w], axis=2)
    rows = rows.reshape(hk, rep, blocks, 4, CH).transpose(0, 2, 1, 3, 4).reshape(hk, blocks, rep * 4, CH)
    docs = ((doc[:, :, None] == doc[:, None, :]) & (tri(False) > 0)[None]).astype(f32)
    masks = jnp.stack(
        [
            jnp.broadcast_to((ext_ids[HALO - d : HALO - d + tokens] == ids).astype(f32)[:, None], (tokens, CH))
            for d in range(1, TAPS)
        ]
    )
    taps = [x.astype(f32) for x in (conv_q, conv_k, conv_v)]

    vw = rep * DK
    col = lambda rows_, width, off=0: pl.BlockSpec((rows_, width), lambda i, off=off, width=width: (0, off // width + i))
    fixed = lambda shape: pl.BlockSpec(shape, lambda i: (0,) * len(shape))
    per = lambda shape: pl.BlockSpec(shape, lambda i: (i,) + (0,) * (len(shape) - 1))
    taps_specs = [col(TAPS, DK), col(TAPS, DK), col(TAPS, vw)]
    common_specs = taps_specs + [
        fixed((TAPS - 1, tokens, CH)),
        fixed((blocks, CH, CH)),
        per((1, blocks, rep * 4, CH)),
    ]
    params = pltpu.CompilerParams(dimension_semantics=("arbitrary",), vmem_limit_bytes=48 * 2**20)
    saved_specs = [
        col(tokens, DK), col(tokens, DK), col(tokens, vw), col(tokens, DK), col(tokens, DK), col(tokens, vw),
        per((1, rep, blocks, CH, CH)), per((1, blocks, CH, CH)), per((1, blocks, CH, CH)),
        per((1, rep, blocks, CH, CH)),
    ]
    saved_shapes = [
        sds((tokens, qw)), sds((tokens, qw)), sds((tokens, hv * DK)), sds((tokens, qw)), sds((tokens, qw)),
        sds((tokens, hv * DK), bf16), sds((hk, rep, blocks, CH, CH)), sds((hk, blocks, CH, CH)),
        sds((hk, blocks, CH, CH)), sds((hk, rep, blocks, CH, CH)),
    ]
    state_spec = per((rep, DK, DK))
    state_shape = sds((hv, DK, DK))
    units = hv * blocks * 2 * 4 * CH**3
    inputs = (flags, q_raw, k_raw, v_raw, out_grad, got, got, got, got, halo, halo, halo, *taps, masks, docs, rows)
    in_specs = [
        pl.BlockSpec(memory_space=pltpu.SMEM),
        col(tokens, DK), col(tokens, DK), col(tokens, vw), col(tokens, vw),
        col(SWAP, DK), col(SWAP, DK, qw), col(SWAP, vw, 2 * qw), col(SWAP, vw, 2 * qw + hv * DK),
        col(HALO, DK), col(HALO, DK, qw), col(HALO, vw, 2 * qw),
    ] + common_specs
    prepare_cost = pl.CostEstimate(flops=22 * units, bytes_accessed=24 * 2**20, transcendentals=2**20)
    if shards // DOC_PARTS == lax.axis_size("pair"):

        def held(spec, lag):
            if spec.index_map is None:
                return spec
            index = spec.index_map
            return pl.BlockSpec(spec.block_shape, lambda i: index(jnp.clip(i - lag, 0, hk - 1)))

        sems = pltpu.SemaphoreType.DMA((hk,))
        states = pltpu.VMEM((hk, rep, DK, DK), f32)
        prepared = pl.pallas_call(
            functools.partial(exchange_kernel, lax.axis_size("ctx"), hk),
            grid=(hk + 3,),
            in_specs=[held(spec, 0) for spec in in_specs],
            out_specs=[held(spec, 0) for spec in saved_specs] + [held(state_spec, 3)] * 2,
            out_shape=saved_shapes + [state_shape] * 2,
            scratch_shapes=[pltpu.VMEM((hk, 2, rep, DK, DK), f32)] * 2 + [states] * 5 + [sems] * 6,
            compiler_params=pltpu.CompilerParams(
                dimension_semantics=("arbitrary",), vmem_limit_bytes=48 * 2**20, collective_id=0,
                has_side_effects=True,
            ),
            cost_estimate=prepare_cost,
            name="exchange",
        )(*inputs)
        saved, (s_in, d_in) = prepared[:10], prepared[10:]
    else:
        prepared = pl.pallas_call(
            prepare_kernel,
            grid=(hk,),
            in_specs=in_specs,
            out_specs=saved_specs + [state_spec] * 3,
            out_shape=saved_shapes + [state_shape] * 3,
            compiler_params=params,
            cost_estimate=prepare_cost,
            name="prepare",
        )(*inputs)
        saved, (m, a, g) = prepared[:10], prepared[10:]
        join = pl.pallas_call(
            join_kernel,
            grid=(hk,),
            in_specs=[state_spec] * 5,
            out_specs=[state_spec] * 2,
            out_shape=[state_shape] * 2,
            compiler_params=params,
            cost_estimate=pl.CostEstimate(flops=hv * 16 * CH**3, bytes_accessed=7 * 2**20, transcendentals=0),
            name="join",
        )
        s_in, d_in = a, g
        for step in range(hops):
            s_in, d_in = shifted(s_in, 1), shifted(d_in, -1)
            if step < hops - 1:
                s_in, d_in = join(m, a, g, s_in, d_in)

    ends = [col(HALO, DK), col(HALO, DK), col(HALO, vw)]
    end_shapes = [sds((HALO, qw)), sds((HALO, qw)), sds((HALO, hv * DK))]
    results = pl.pallas_call(
        main_kernel,
        grid=(hk,),
        in_specs=saved_specs + common_specs + [state_spec] * 2,
        out_specs=[col(tokens, vw), col(tokens, DK), col(tokens, DK), col(tokens, vw)] + ends + ends + [per((1, blocks, 8, CH))],
        out_shape=[
            sds((tokens, hv * DK), bf16), sds((tokens, qw), bf16), sds((tokens, qw), bf16), sds((tokens, hv * DK), bf16)
        ] + end_shapes + end_shapes + [sds((hk, blocks, 8, CH))],
        compiler_params=params,
        cost_estimate=pl.CostEstimate(flops=17 * units, bytes_accessed=24 * 2**20, transcendentals=2**20),
        name="main",
    )(*saved, *taps, masks, docs, rows, s_in, d_in)
    layer_out, q_grad, k_grad, v_grad = results[:4]
    spilled = shifted(jnp.concatenate(results[7:10], axis=1), -1)
    ends_out = []
    at = 0
    for grad, end in zip((q_grad, k_grad, v_grad), results[4:7]):
        width = end.shape[1]
        last = (end + spilled[:, at : at + width]).astype(bf16)
        ends_out.append(lax.dynamic_update_slice(grad, last, (tokens - HALO, 0)))
        at += width
    rg = results[10][:, :, : 2 * rep].reshape(hk, blocks, rep, 2, CH).transpose(3, 0, 2, 1, 4)
    dbeta = rg[0].reshape(hv, tokens)
    dg = jnp.dot(rg[1].reshape(hv * blocks, CH), tri(False), precision=highest).reshape(hv, tokens)
    beta_grad = dbeta * beta * (1.0 - beta)
    gate_grad = dg * rate * jax.nn.sigmoid(gate)
    return (layer_out, ends_out[0], ends_out[1], ends_out[2], beta_grad.astype(bf16), gate_grad.astype(bf16))


def solution(mesh):
    rows = P(("groups", "ctx", "pair"), "head")
    rates = P("head", ("groups", "ctx", "pair"))
    taps = P(None, "head")
    return jax.shard_map(
        body,
        mesh=mesh,
        in_specs=(
            rows, rows, rows, rates, rates, rows, taps, taps, taps, P("head"), P("head"),
            P(("groups", "ctx", "pair")), P(("groups", "ctx")),
        ),
        out_specs=(rows, rows, rows, rows, rates, rates),
        check_vma=False,
    )
```
